32 devices in a mesh: dp: 4 (over y, x), tensor: 8 (over z, core).
Axes of the slice: x: 2, y: 2, z: 4, core: 2. Of those that a mesh axis runs over, the one named last changes fastest.
Arguments:
- grad_out: bfloat16 [4096, 8192], P('dp', 'tensor'), may hold values from -6 to 6
- acts: bfloat16 [4096, 16384], P('dp', 'tensor'), may hold values from -6 to 6
- weight: bfloat16 [8192, 16384], P('tensor'), may hold values from -0.078125 to 0.078125
- block_mask: int32 [64, 128], replicated, may hold values from 0 to 1, as said below
Outputs:
- grad_acts: bfloat16 [4096, 16384], P('dp', 'tensor')
- grad_weight: float32 [8192, 16384], P(('dp', 'tensor'))
The draws below stay inside these ranges and needn't reach their ends.
Inputs may be any that keep to these rules, and one draw needn't show every extreme that they name: `block_mask`: kept shares differ between groups of 16 consecutive block columns, from about three twentieths to nine twentieths.
All inputs are finite; a program needn't handle non-finite values.
Results may differ from the reference program's by a relative error of at most 0.001.
Values may be sent and summed in bfloat16 or wider, within the bound.
No kernel may reach another device: no remote copies, remote signals or barrier semaphores. Data moves between devices by JAX's collectives and lax.ppermute only.
A program may use at most 320 MiB of HBM per device.

```python
import jax
import jax.numpy as jnp
from jax import lax

D = 8192
FF = 16384
BLK = 128
TOKENS = 4096
FF_TILE = 2048


def draw_block_mask(key, part):
    rows = D // BLK
    cols = FF // BLK
    per_tile = FF_TILE // BLK
    groups = cols // per_tile
    first_key, second_key = jax.random.split(jax.random.fold_in(key, 11))
    order = jax.random.permutation(first_key, groups).astype(jnp.int32)
    level = 3 + order * 7 // groups
    level = jnp.repeat(level, per_tile)
    picks = jax.random.randint(second_key, (rows, cols), 0, 20)
    return (picks < level[None, :]).astype(jnp.int32)


def steps_of(key, dims, cuts, low, top_value):
    factor_of, own = 1.0, jax.random.fold_in(key, 6)
    for dim, shards_of in cuts:
        steps = jnp.exp(jax.random.uniform(jax.random.fold_in(own, dim), (shards_of,), jnp.float32, low / len(cuts), top_value / len(cuts)))
        factor_of = factor_of * jnp.repeat(steps, dims[dim] // shards_of).reshape([-1 if axis == dim else 1 for axis in range(len(dims))])
    return factor_of


def bell_draw(key, extent, scale, limit, cuts=(), kind=jnp.bfloat16):
    values = jax.random.normal(key, extent, jnp.float32) * scale
    if len(cuts) > 0:
        values = steps_of(key, extent, cuts, -0.22, 0.18) * values
    return jnp.clip(values, min=-limit, max=limit).astype(kind)


def setup_inputs(seed: int = 0) -> dict:
    splits = jax.random.split(jax.random.key(seed), 5)
    return {
        "grad_out": bell_draw(splits[0], (TOKENS, D), 1.0, 6.0, ((0, 4), (1, 8))),
        "acts": bell_draw(splits[1], (TOKENS, FF), 1.0, 6.0, ((0, 4), (1, 8))),
        "weight": bell_draw(splits[2], (D, FF), (FF // 3) ** -0.5, 0.078125, ((0, 8),)),
        "block_mask": draw_block_mask(jax.random.fold_in(splits[4], 71), 0),
    }


def expand_mask(mask, side):
    rows, cols = mask.shape
    full = jnp.broadcast_to(mask[:, None, :, None], (rows, side, cols, side))
    return full.reshape(rows * side, cols * side)


def reference(grad_out, acts, weight, block_mask):
    full_mask = expand_mask(block_mask, BLK).astype(jnp.bfloat16)
    kept = weight * full_mask
    grad_acts = jnp.dot(grad_out.astype(jnp.float32), kept.astype(jnp.float32), preferred_element_type=jnp.float32)
    grad_acts = grad_acts.astype(jnp.bfloat16)
    product = lax.dot_general(grad_out.astype(jnp.float32), acts.astype(jnp.float32), (((0,), (0,)), ((), ())), preferred_element_type=jnp.float32)
    grad_weight = product * full_mask.astype(jnp.float32) * (1.0 / (TOKENS ** 0.5))
    return grad_acts, grad_weight
```

```python
import jax
import jax.numpy as jnp
from jax import lax
from jax.experimental import pallas as pl
from jax.experimental.pallas import tpu as pltpu
from jax.sharding import PartitionSpec as P

BF16, F32 = jnp.bfloat16, jnp.float32


def ranks(flags):
    n = flags.shape[1]
    before = jnp.arange(n)[:, None] < jnp.arange(n)[None, :]
    return jnp.sum(flags[:, :, None] * before[None], 1)


def slots_to_send(flags, cap, turn):
    n = flags.shape[1]
    wanted = jnp.arange(cap)[None, :, None] + turn * cap
    hit = (ranks(flags)[:, None, :] == wanted) & (flags[:, None, :] > 0)
    return jnp.sum(jnp.where(hit, jnp.arange(n)[None, None, :], 0), 2)


def slots_received(flags, cap, turn):
    slot = ranks(flags) - turn * cap
    return jnp.where((flags > 0) & (slot >= 0) & (slot < cap), slot, -1)


def pack(source, picked, which, shape):
    tiles, cap, height, side, share, ff_tile = shape
    across = ff_tile // side
    by_column = source.shape[1] != ff_tile

    def kernel(which_ref, row_ref, col_ref, in_ref, out_ref):
        base = pl.program_id(0) * cap
        for s in range(cap):
            row = pl.multiple_of(row_ref[base + s], height)
            col = pl.multiple_of(col_ref[base + s], side)
            out_ref[0, s] = in_ref[pl.ds(row, height), pl.ds(col, side)]

    picked = picked.reshape(-1)
    rows, cols = (picked // across) * height, (picked % across) * side
    if by_column:
        place = lambda t, w, r, c: (w[0], t)
    else:
        place = lambda t, w, r, c: (t, 0)
    return pl.pallas_call(
        kernel,
        out_shape=jax.ShapeDtypeStruct((tiles, cap, height, side), source.dtype),
        grid_spec=pltpu.PrefetchScalarGridSpec(
            num_scalar_prefetch=3,
            grid=(tiles,),
            in_specs=[pl.BlockSpec((share, ff_tile), place)],
            out_specs=pl.BlockSpec((1, cap, height, side), lambda t, w, r, c: (t, 0, 0, 0)),
        ),
        cost_estimate=pl.CostEstimate(
            flops=0, transcendentals=0,
            bytes_accessed=2 * tiles * share * ff_tile * source.dtype.itemsize,
        ),
        name="pack",
    )(which.reshape(1).astype(jnp.int32), rows.astype(jnp.int32), cols.astype(jnp.int32), source)


def unpack(blocks, table, share, ff_tile):
    tiles, cap, height, side = blocks.shape
    across = ff_tile // side
    n = table.shape[1]

    def kernel(table_ref, in_ref, out_ref):
        base = pl.program_id(0) * n
        for p in range(n):
            slot = table_ref[base + p]
            value = in_ref[0, jnp.maximum(slot, 0)]
            row, col = (p // across) * height, (p % across) * side
            out_ref[row:row + height, col:col + side] = jnp.where(slot >= 0, value, jnp.zeros_like(value))

    return pl.pallas_call(
        kernel,
        out_shape=jax.ShapeDtypeStruct((share, tiles * ff_tile), blocks.dtype),
        grid_spec=pltpu.PrefetchScalarGridSpec(
            num_scalar_prefetch=1,
            grid=(tiles,),
            in_specs=[pl.BlockSpec((1, cap, height, side), lambda t, s: (t, 0, 0, 0))],
            out_specs=pl.BlockSpec((share, ff_tile), lambda t, s: (0, t)),
        ),
        cost_estimate=pl.CostEstimate(
            flops=0, transcendentals=0, bytes_accessed=8 * tiles * share * ff_tile,
        ),
        name="unpack",
    )(table.reshape(-1).astype(jnp.int32), blocks)


def accumulate(total, features, index, sources, table, share, ff_tile, out_type):
    tiles, tokens = table.shape[0], features.shape[1]
    _, cap, height, side = sources[0][0].shape
    n = table.shape[1]
    across = ff_tile // side
    direct = share % 128 == 0
    cut = tiles // 2
    together = min(cut, max(1, 256 // share))
    depth = together * share
    step = min(tokens, 256)
    steps = cut // together

    def kernel(index_ref, table_ref, *refs):
        lefts, blocks, (total_ref, out_ref, strip, sums) = refs[:2], refs[2:4], refs[4:]

        @pl.when(pl.program_id(0) == 0)
        def _():
            sums[...] = total_ref[...]

        for stream in range(2):
            base = (stream * cut + pl.program_id(0) * together) * n
            for t in range(together):
                for p in range(n):
                    slot = table_ref[base + t * n + p]
                    value = blocks[stream][t, jnp.maximum(slot, 0)]
                    row, col = t * share + (p // across) * height, (p % across) * side
                    strip[stream, row:row + height, col:col + side] = jnp.where(
                        slot >= 0, value, jnp.zeros_like(value)
                    )

        @pl.loop(0, tokens // step)
        def _(m):
            at = pl.ds(pl.multiple_of(m * step, step), step)
            value = sums[at]
            for stream in range(2):
                for t in range(together if direct else 1):
                    size = share if direct else depth
                    value += jnp.dot(
                        lefts[stream][t, at], strip[stream, t * size:(t + 1) * size],
                        preferred_element_type=F32,
                    )
            sums[at] = value

        @pl.when(pl.program_id(0) == steps - 1)
        def _():
            out_ref[...] = sums[...].astype(out_type)

    def left(stream):
        if direct:
            return pl.BlockSpec(
                (together, tokens, share), lambda i, e, s: (stream * steps + i, 0, e[0])
            )
        return pl.BlockSpec((1, tokens, depth), lambda i, e, s: (e[0], 0, stream * steps + i))

    def block(first):
        return pl.BlockSpec(
            (together, cap, height, side), lambda i, e, s: (first // together + i, 0, 0, 0)
        )

    whole = pl.BlockSpec((tokens, ff_tile), lambda i, e, s: (0, 0), pipeline_mode=pl.Buffered(1))
    return pl.pallas_call(
        kernel,
        out_shape=jax.ShapeDtypeStruct((tokens, ff_tile), out_type),
        grid_spec=pltpu.PrefetchScalarGridSpec(
            num_scalar_prefetch=2,
            grid=(steps,),
            in_specs=[left(0), left(1)] + [block(first) for _, first in sources] + [whole],
            out_specs=pl.BlockSpec((tokens, ff_tile), lambda i, e, s: (0, 0)),
            scratch_shapes=[
                pltpu.VMEM((2, depth, ff_tile), BF16), pltpu.VMEM((tokens, ff_tile), F32)
            ],
        ),
        cost_estimate=pl.CostEstimate(
            flops=2 * tokens * tiles * share * ff_tile, transcendentals=0,
            bytes_accessed=2 * tokens * tiles * share + 8 * tokens * ff_tile,
        ),
        name="accumulate",
    )(
        index.reshape(1).astype(jnp.int32), table.reshape(-1).astype(jnp.int32),
        features, features, sources[0][0], sources[1][0], total,
    )


def pairs(count, flip):
    return [(i, i ^ flip) for i in range(count)]


def body(grad_out, acts, weight, block_mask):
    groups = lax.axis_size("dp")
    tiles = lax.axis_size("tensor")
    group = lax.axis_index("dp")
    position = lax.axis_index("tensor")
    tokens, d_tile = grad_out.shape
    ff_tile = acts.shape[1]
    side = weight.shape[1] // block_mask.shape[1]
    share = d_tile // groups
    per = tiles // groups
    rows = per * d_tile
    height = min(side, share)
    down, across = share // height, ff_tile // side
    n = down * across
    cap = -(-3 * n // 4)
    shape = (tiles, cap, height, side, share, ff_tile)

    units = jnp.repeat(block_mask, side // height, axis=0)
    by_weight = units.reshape(tiles, groups, down, tiles, across)
    by_output = units.reshape(groups, tiles, down, tiles, across)
    turns = -(-jnp.maximum(jnp.max(jnp.sum(by_weight, (2, 4))), jnp.max(jnp.sum(by_output, (2, 4)))) // cap)

    def at(array, *where):
        for axis, index in where:
            array = lax.dynamic_index_in_dim(array, index, axis, keepdims=True)
        return array

    weight_out = at(by_weight, (0, position), (1, group))[0, 0].transpose(1, 0, 2).reshape(tiles, n)
    weight_in = at(by_weight, (3, position))[:, :, :, 0].transpose(1, 0, 2, 3).reshape(groups, tiles, n)
    result_out = at(by_output, (0, group), (3, position))[0, :, :, 0].reshape(tiles, n)
    result_in = at(by_output, (0, group), (1, position))[0, 0].transpose(1, 0, 2).reshape(tiles, n)

    def hops(array, flips, axis="dp", count=groups):
        return [lax.ppermute(array(f), axis, pairs(count, f)) for f in flips]

    other_acts = hops(lambda f: acts, (1, 2, 3))
    features = lax.all_gather(grad_out, "tensor", axis=0, tiled=False)

    def packed_weight(turn):
        return pack(weight, slots_to_send(weight_out, cap, turn), group, shape)

    def exchange(array):
        return lax.all_to_all(array, "tensor", split_axis=0, concat_axis=0, tiled=True)

    own, features = lax.optimization_barrier((packed_weight(0), features))
    own = exchange(own)

    core = position % 2
    half = per // 2

    def chosen(flip):
        start = (group ^ flip) * per + core * half
        return lax.dynamic_slice_in_dim(features, start, half, 0)

    got = hops(chosen, (1, 2, 3))
    other = [lax.ppermute(piece, "tensor", pairs(tiles, 1)) for piece in got]
    mine = lax.dynamic_slice_in_dim(features, group * per, per, 0)
    low = [jnp.where(core == 0, a, b) for a, b in zip(got, other)]
    high = [jnp.where(core == 0, b, a) for a, b in zip(got, other)]
    left = jnp.concatenate([mine] + [jnp.concatenate([a, b], 0) for a, b in zip(low, high)], 1)
    right = jnp.concatenate([acts] + other_acts, 0)
    product = jnp.einsum("ptf,th->pfh", left, right, preferred_element_type=F32)
    product = product.reshape(rows, ff_tile)
    scale_factor = 1.0 / (tokens * groups) ** 0.5

    def moved_product(turn):
        blocks = pack(product, slots_to_send(result_out, cap, turn), group, shape)
        blocks = blocks.reshape(tiles, cap * height, side)
        top = jnp.max(jnp.abs(blocks), (1, 2)) * scale_factor
        power = jnp.ceil(jnp.log2(jnp.where(top > 0, top, 1.0)))
        power = jnp.clip(power, -110.0, 110.0) - 12.0
        sent = (blocks * (scale_factor * jnp.exp2(-power))[:, None, None]).astype(jnp.float16)
        note = jnp.broadcast_to(power[:, None, None], (tiles, 16, side)).astype(jnp.float16)
        sent = jnp.concatenate([sent, note], 1)
        got = exchange(sent)
        power = got[:, cap * height, 0].astype(F32)
        blocks = got[:, :cap * height].astype(F32) * jnp.exp2(power)[:, None, None]
        blocks = blocks.reshape(tiles, cap, height, side)
        return unpack(blocks, slots_received(result_in, cap, turn), share, ff_tile)

    grad_weight = moved_product(0)

    if share % 128 == 0:
        lefts = features
    else:
        lefts = features.reshape(tiles, tokens, groups, share).transpose(2, 1, 0, 3)
        lefts = lefts.reshape(groups, tokens, tiles * share)
    cut = tiles // 2

    def add(total, index, sources, turn, out_type=F32):
        table = slots_received(lax.dynamic_index_in_dim(weight_in, index, 0, keepdims=False), cap, turn)
        return accumulate(total, lefts, index, sources, table, share, ff_tile, out_type)

    def more_acts(carry):
        turn, total = carry
        pieces = lax.all_gather(exchange(packed_weight(turn)), "dp", axis=0, tiled=False)

        def one(e, total):
            piece = lax.dynamic_index_in_dim(pieces, e, 0, keepdims=False)
            return add(total, e, ((piece, 0), (piece, cut)), turn)

        return turn + 1, lax.fori_loop(0, groups, one, total)

    def more_weight(carry):
        turn, total = carry
        return turn + 1, total + moved_product(turn)

    def unfinished(carry):
        return carry[0] < turns

    total = jnp.zeros((tokens, ff_tile), F32)
    _, total = lax.while_loop(unfinished, more_acts, (jnp.int32(1), total))
    _, grad_weight = lax.while_loop(unfinished, more_weight, (jnp.int32(1), grad_weight))

    near_x, near_y = hops(lambda f: own, (1, 2))
    far_low = lax.ppermute(near_x[:cut], "dp", pairs(groups, 2))
    far_high = lax.ppermute(near_y[cut:], "dp", pairs(groups, 1))
    total = add(total, group, ((own, 0), (own, cut)), 0)
    total = add(total, group ^ 1, ((near_x, 0), (near_x, cut)), 0)
    total = add(total, group ^ 2, ((near_y, 0), (near_y, cut)), 0)
    total = add(total, group ^ 3, ((far_low, 0), (far_high, 0)), 0, BF16)
    return total, grad_weight


def solution(mesh):
    in_specs = (P("dp", "tensor"), P("dp", "tensor"), P("tensor", None), P())
    out_specs = (P("dp", "tensor"), P(("dp", "tensor"), None))
    return jax.shard_map(body, mesh=mesh, in_specs=in_specs, out_specs=out_specs, check_vma=False)
```

```python
import jax
import jax.numpy as jnp
from jax import lax
from jax.experimental import pallas as pl
from jax.experimental.pallas import tpu as pltpu
from jax.sharding import PartitionSpec as P

BF16, F32 = jnp.bfloat16, jnp.float32


def ranks(flags):
    n = flags.shape[1]
    before = jnp.arange(n)[:, None] < jnp.arange(n)[None, :]
    return jnp.sum(flags[:, :, None] * before[None], 1)


def slots_to_send(flags, size, first):
    n = flags.shape[1]
    wanted = jnp.arange(size)[None, :, None] + first
    hit = (ranks(flags)[:, None, :] == wanted) & (flags[:, None, :] > 0)
    return jnp.sum(jnp.where(hit, jnp.arange(n)[None, None, :], 0), 2)


def slots_received(flags, cap, turn):
    slot = ranks(flags) - turn * cap
    return jnp.where((flags > 0) & (slot >= 0) & (slot < cap), slot, -1)


def pack(source, picked, which, shape):
    tiles, cap, height, side, share, ff_tile = shape
    across = ff_tile // side

    def kernel(which_ref, row_ref, col_ref, in_ref, out_ref):
        base = pl.program_id(0) * cap
        for s in range(cap):
            row = pl.multiple_of(row_ref[base + s], height)
            col = pl.multiple_of(col_ref[base + s], side)
            out_ref[0, s] = in_ref[pl.ds(row, height), pl.ds(col, side)]

    picked = picked.reshape(-1)
    rows, cols = (picked // across) * height, (picked % across) * side
    return pl.pallas_call(
        kernel,
        out_shape=jax.ShapeDtypeStruct((tiles, cap, height, side), source.dtype),
        grid_spec=pltpu.PrefetchScalarGridSpec(
            num_scalar_prefetch=3,
            grid=(tiles,),
            in_specs=[pl.BlockSpec((share, ff_tile), lambda t, w, r, c: (w[0], t))],
            out_specs=pl.BlockSpec((1, cap, height, side), lambda t, w, r, c: (t, 0, 0, 0)),
        ),
        cost_estimate=pl.CostEstimate(
            flops=0, transcendentals=0,
            bytes_accessed=2 * tiles * share * ff_tile * source.dtype.itemsize,
        ),
        name="pack",
    )(which.reshape(1).astype(jnp.int32), rows.astype(jnp.int32), cols.astype(jnp.int32), source)


def pack_scaled(first, second, picked, core, factor, shape):
    tiles, cap, height, side, share, ff_tile = shape
    across = ff_tile // side
    half = tiles // 2

    def kernel(core_ref, row_ref, col_ref, first_ref, second_ref, out_ref):
        tile = pl.program_id(0)
        base = tile * cap
        swapped = (tile >= half).astype(jnp.int32) != core_ref[0]

        def run(in_ref):
            def block(s):
                row = pl.multiple_of(row_ref[base + s], height)
                col = pl.multiple_of(col_ref[base + s], side)
                return in_ref[pl.ds(row, height), pl.ds(col, side)]

            top = lax.fori_loop(
                0, cap, lambda s, top: jnp.maximum(top, jnp.abs(block(s))),
                jnp.zeros((height, side), F32),
            )
            top = jnp.full((16, side), jnp.max(top) * factor, F32)
            power = jnp.ceil(jnp.log2(jnp.where(top > 0, top, 1.0)))
            power = jnp.clip(power, -110.0, 110.0) - 12.0
            scale = jnp.exp2(-power)[:1] * factor

            @pl.loop(0, cap)
            def _(s):
                out_ref[0, pl.ds(pl.multiple_of(s * height, height), height)] = block(s) * scale

            out_ref[0, cap * height:] = power

        pl.when(jnp.logical_not(swapped))(lambda: run(first_ref))
        pl.when(swapped)(lambda: run(second_ref))

    def place(second_half):
        def index(t, w, r, c):
            spot = (t + w[0] * half) % tiles
            return (jnp.clip(spot - half, 0, half - 1) if second_half else jnp.minimum(spot, half - 1), 0)

        return pl.BlockSpec((share, ff_tile), index)

    picked = picked.reshape(-1)
    rows, cols = (picked // across) * height, (picked % across) * side
    return pl.pallas_call(
        kernel,
        out_shape=jax.ShapeDtypeStruct((tiles, cap * height + 16, side), F32),
        grid_spec=pltpu.PrefetchScalarGridSpec(
            num_scalar_prefetch=3,
            grid=(tiles,),
            in_specs=[place(False), place(True)],
            out_specs=pl.BlockSpec((1, cap * height + 16, side), lambda t, w, r, c: (t, 0, 0)),
        ),
        cost_estimate=pl.CostEstimate(
            flops=0, transcendentals=0, bytes_accessed=8 * tiles * share * ff_tile,
        ),
        name="pack_scaled",
    )(core.reshape(1).astype(jnp.int32), rows.astype(jnp.int32), cols.astype(jnp.int32), first, second)


def unpack(blocks, table, share, ff_tile):
    tiles, cap, height, side = blocks.shape
    across = ff_tile // side
    n = table.shape[1]

    def kernel(table_ref, in_ref, out_ref):
        base = pl.program_id(0) * n
        for p in range(n):
            slot = table_ref[base + p]
            value = in_ref[0, jnp.maximum(slot, 0)]
            row, col = (p // across) * height, (p % across) * side
            out_ref[row:row + height, col:col + side] = jnp.where(slot >= 0, value, jnp.zeros_like(value))

    return pl.pallas_call(
        kernel,
        out_shape=jax.ShapeDtypeStruct((share, tiles * ff_tile), blocks.dtype),
        grid_spec=pltpu.PrefetchScalarGridSpec(
            num_scalar_prefetch=1,
            grid=(tiles,),
            in_specs=[pl.BlockSpec((1, cap, height, side), lambda t, s: (t, 0, 0, 0))],
            out_specs=pl.BlockSpec((share, ff_tile), lambda t, s: (0, t)),
        ),
        cost_estimate=pl.CostEstimate(
            flops=0, transcendentals=0, bytes_accessed=8 * tiles * share * ff_tile,
        ),
        name="unpack",
    )(table.reshape(-1).astype(jnp.int32), blocks)


def accumulate(total, features, index, sources, table, share, ff_tile, out_type):
    tiles, tokens = table.shape[0], features.shape[1]
    parts = [part.shape[1] for part in sources[0][0]]
    height, side = sources[0][0][0].shape[2:]
    n = table.shape[1]
    across = ff_tile // side
    direct = share % 128 == 0
    cut = tiles // 2
    together = min(cut, max(1, 256 // share))
    depth = together * share
    step = min(tokens, 256)
    steps = cut // together

    def kernel(index_ref, table_ref, *refs):
        lefts, (total_ref, out_ref, strip, sums) = refs[:2], refs[-4:]
        blocks = refs[2:2 + len(parts)], refs[2 + len(parts):-4]

        def kept(stream, t, slot):
            value = blocks[stream][0][t, jnp.clip(slot, 0, parts[0] - 1)]
            before = parts[0]
            for size, ref in zip(parts[1:], blocks[stream][1:]):
                later = ref[t, jnp.clip(slot - before, 0, size - 1)]
                value = jnp.where(slot >= before, later, value)
                before += size
            return jnp.where(slot >= 0, value, jnp.zeros_like(value))

        @pl.when(pl.program_id(0) == 0)
        def _():
            sums[...] = total_ref[...]

        for stream in range(2):
            base = (stream * cut + pl.program_id(0) * together) * n
            for t in range(together):
                for p in range(n):
                    slot = table_ref[base + t * n + p]
                    row, col = t * share + (p // across) * height, (p % across) * side
                    strip[stream, row:row + height, col:col + side] = kept(stream, t, slot)

        @pl.loop(0, tokens // step)
        def _(m):
            at = pl.ds(pl.multiple_of(m * step, step), step)
            value = sums[at]
            for stream in range(2):
                for t in range(together if direct else 1):
                    size = share if direct else depth
                    value += jnp.dot(
                        lefts[stream][t, at], strip[stream, t * size:(t + 1) * size],
                        preferred_element_type=F32,
                    )
            sums[at] = value

        @pl.when(pl.program_id(0) == steps - 1)
        def _():
            out_ref[...] = sums[...].astype(out_type)

    def left(stream):
        if direct:
            return pl.BlockSpec(
                (together, tokens, share), lambda i, e, s: (stream * steps + i, 0, e[0])
            )
        return pl.BlockSpec((1, tokens, depth), lambda i, e, s: (e[0], 0, stream * steps + i))

    def block(size, first):
        return pl.BlockSpec(
            (together, size, height, side), lambda i, e, s: (first // together + i, 0, 0, 0)
        )

    whole = pl.BlockSpec((tokens, ff_tile), lambda i, e, s: (0, 0), pipeline_mode=pl.Buffered(1))
    return pl.pallas_call(
        kernel,
        out_shape=jax.ShapeDtypeStruct((tokens, ff_tile), out_type),
        grid_spec=pltpu.PrefetchScalarGridSpec(
            num_scalar_prefetch=2,
            grid=(steps,),
            in_specs=[left(0), left(1)]
            + [block(size, first) for _, first in sources for size in parts] + [whole],
            out_specs=pl.BlockSpec((tokens, ff_tile), lambda i, e, s: (0, 0)),
            scratch_shapes=[
                pltpu.VMEM((2, depth, ff_tile), BF16), pltpu.VMEM((tokens, ff_tile), F32)
            ],
        ),
        cost_estimate=pl.CostEstimate(
            flops=2 * tokens * tiles * share * ff_tile, transcendentals=0,
            bytes_accessed=2 * tokens * tiles * share + 8 * tokens * ff_tile,
        ),
        name="accumulate",
    )(
        index.reshape(1).astype(jnp.int32), table.reshape(-1).astype(jnp.int32),
        features, features, *sources[0][0], *sources[1][0], total,
    )


def pairs(count, flip):
    return [(i, i ^ flip) for i in range(count)]


def body(grad_out, acts, weight, block_mask):
    groups = lax.axis_size("dp")
    tiles = lax.axis_size("tensor")
    group = lax.axis_index("dp")
    position = lax.axis_index("tensor")
    tokens, d_tile = grad_out.shape
    ff_tile = acts.shape[1]
    side = weight.shape[1] // block_mask.shape[1]
    share = d_tile // groups
    per = tiles // groups
    rows = per * d_tile
    height = min(side, share)
    down, across = share // height, ff_tile // side
    n = down * across
    cap = -(-3 * n // 4)
    parts = [cap // 2, cap - cap // 2] if cap > 1 else [cap]
    shape = (tiles, cap, height, side, share, ff_tile)

    units = jnp.repeat(block_mask, side // height, axis=0)
    by_weight = units.reshape(tiles, groups, down, tiles, across)
    by_output = units.reshape(groups, tiles, down, tiles, across)
    turns = -(-jnp.maximum(jnp.max(jnp.sum(by_weight, (2, 4))), jnp.max(jnp.sum(by_output, (2, 4)))) // cap)

    def at(array, *where):
        for axis, index in where:
            array = lax.dynamic_index_in_dim(array, index, axis, keepdims=True)
        return array

    weight_out = at(by_weight, (0, position), (1, group))[0, 0].transpose(1, 0, 2).reshape(tiles, n)
    weight_in = at(by_weight, (3, position))[:, :, :, 0].transpose(1, 0, 2, 3).reshape(groups, tiles, n)
    result_out = at(by_output, (0, group), (3, position))[0, :, :, 0].reshape(tiles, n)
    result_in = at(by_output, (0, group), (1, position))[0, 0].transpose(1, 0, 2).reshape(tiles, n)

    def hops(array, flips, axis="dp", count=groups):
        return [lax.ppermute(array(f), axis, pairs(count, f)) for f in flips]

    acts_x, acts_y = hops(lambda f: acts, (1, 2))
    acts_low = lax.ppermute(acts_x[:tokens // 2], "dp", pairs(groups, 2))
    acts_high = lax.ppermute(acts_y[tokens // 2:], "dp", pairs(groups, 1))
    features = lax.all_gather(grad_out, "tensor", axis=0, tiled=False)

    def packed_weight(turn):
        made, first = [], turn * cap
        for size in parts:
            picked = slots_to_send(weight_out, size, first)
            made.append(pack(weight, picked, group, (tiles, size) + shape[2:]))
            first = first + size
        return made

    def exchange(array):
        return lax.all_to_all(array, "tensor", split_axis=0, concat_axis=0, tiled=True)

    own = packed_weight(0)
    own, features = lax.optimization_barrier((own, features))
    for i, part in enumerate(own):
        own[i] = exchange(part)

    core = position % 2
    half = per // 2

    def chosen(flip, which=core):
        start = (group ^ flip) * per + which * half
        return lax.dynamic_slice_in_dim(features, start, half, 0)

    got = hops(chosen, (1, 2, 3))
    other = [lax.ppermute(piece, "tensor", pairs(tiles, 1)) for piece in got]

    def contract(left, right):
        out = jnp.einsum("ptf,th->pfh", left, right, preferred_element_type=F32)
        return out.reshape(rows // 2, ff_tile)

    products = []
    for pieces in ([chosen(0)] + got, [chosen(0, 1 - core)] + other):
        product = contract(pieces[0], acts)
        product = product + contract(pieces[1], acts_x)
        product = product + contract(pieces[2], acts_y)
        far = jnp.concatenate([acts_low, acts_high], 0)
        product = product + contract(pieces[3], far)
        products.append(product)
    scale_factor = 1.0 / (tokens * groups) ** 0.5

    def moved_product(turn):
        picked = slots_to_send(result_out, cap, turn * cap)
        sent = pack_scaled(*products, picked, core, scale_factor, shape).astype(jnp.float16)
        got = exchange(sent)
        power = got[:, cap * height, 0].astype(F32)
        blocks = got[:, :cap * height].astype(F32) * jnp.exp2(power)[:, None, None]
        blocks = blocks.reshape(tiles, cap, height, side)
        return unpack(blocks, slots_received(result_in, cap, turn), share, ff_tile)

    grad_weight = moved_product(0)

    if share % 128 == 0:
        lefts = features
    else:
        lefts = features.reshape(tiles, tokens, groups, share).transpose(2, 1, 0, 3)
        lefts = lefts.reshape(groups, tokens, tiles * share)
    cut = tiles // 2

    def add(total, index, sources, turn, out_type=F32):
        table = slots_received(lax.dynamic_index_in_dim(weight_in, index, 0, keepdims=False), cap, turn)
        return accumulate(total, lefts, index, sources, table, share, ff_tile, out_type)

    def more_acts(carry):
        turn, total = carry
        pieces = [lax.all_gather(exchange(p), "dp", axis=0, tiled=False) for p in packed_weight(turn)]

        def one(e, total):
            piece = [lax.dynamic_index_in_dim(p, e, 0, keepdims=False) for p in pieces]
            return add(total, e, ((piece, 0), (piece, cut)), turn)

        return turn + 1, lax.fori_loop(0, groups, one, total)

    def more_weight(carry):
        turn, total = carry
        return turn + 1, total + moved_product(turn)

    def unfinished(carry):
        return carry[0] < turns

    total = jnp.zeros((tokens, ff_tile), F32)
    _, total = lax.while_loop(unfinished, more_acts, (jnp.int32(1), total))
    _, grad_weight = lax.while_loop(unfinished, more_weight, (jnp.int32(1), grad_weight))

    near_x, near_y, far_low, far_high = [], [], [], []
    for part in own:
        x, y = hops(lambda f: part, (1, 2))
        far_low.append(lax.ppermute(x[:cut], "dp", pairs(groups, 2)))
        far_high.append(lax.ppermute(y[cut:], "dp", pairs(groups, 1)))
        near_x.append(x)
        near_y.append(y)
    total = add(total, group, ((own, 0), (own, cut)), 0)
    total = add(total, group ^ 1, ((near_x, 0), (near_x, cut)), 0)
    total = add(total, group ^ 2, ((near_y, 0), (near_y, cut)), 0)
    total = add(total, group ^ 3, ((far_low, 0), (far_high, 0)), 0, BF16)
    return total, grad_weight


def solution(mesh):
    in_specs = (P("dp", "tensor"), P("dp", "tensor"), P("tensor", None), P())
    out_specs = (P("dp", "tensor"), P(("dp", "tensor"), None))
    return jax.shard_map(body, mesh=mesh, in_specs=in_specs, out_specs=out_specs, check_vma=False)
```

```python
import jax
import jax.numpy as jnp
from jax import lax
from jax.experimental import pallas as pl
from jax.experimental.pallas import tpu as pltpu
from jax.sharding import PartitionSpec as P

BF16, F32 = jnp.bfloat16, jnp.float32


def ranks(flags):
    n = flags.shape[1]
    before = jnp.arange(n)[:, None] < jnp.arange(n)[None, :]
    return jnp.sum(flags[:, :, None] * before[None], 1)


def slots_to_send(flags, size, first):
    n = flags.shape[1]
    wanted = jnp.arange(size)[None, :, None] + first
    hit = (ranks(flags)[:, None, :] == wanted) & (flags[:, None, :] > 0)
    return jnp.sum(jnp.where(hit, jnp.arange(n)[None, None, :], 0), 2)


def slots_received(flags, cap, turn):
    slot = ranks(flags) - turn * cap
    return jnp.where((flags > 0) & (slot >= 0) & (slot < cap), slot, -1)


def place(p, across, height, side):
    row = pl.multiple_of(lax.div(p, across) * height, height)
    col = pl.multiple_of(lax.rem(p, across) * side, side)
    return pl.ds(row, height), pl.ds(col, side)


def pack(source, picked, which, shape):
    tiles, cap, height, side, share, ff_tile = shape
    across = ff_tile // side

    def kernel(which_ref, row_ref, col_ref, in_ref, out_ref):
        base = pl.program_id(0) * cap

        @pl.loop(0, cap)
        def _(s):
            row = pl.multiple_of(row_ref[base + s], height)
            col = pl.multiple_of(col_ref[base + s], side)
            out_ref[0, s] = in_ref[pl.ds(row, height), pl.ds(col, side)]

    picked = picked.reshape(-1)
    rows, cols = (picked // across) * height, (picked % across) * side
    return pl.pallas_call(
        kernel,
        out_shape=jax.ShapeDtypeStruct((tiles, cap, height, side), source.dtype),
        grid_spec=pltpu.PrefetchScalarGridSpec(
            num_scalar_prefetch=3,
            grid=(tiles,),
            in_specs=[pl.BlockSpec((share, ff_tile), lambda t, w, r, c: (w[0], t))],
            out_specs=pl.BlockSpec((1, cap, height, side), lambda t, w, r, c: (t, 0, 0, 0)),
        ),
        cost_estimate=pl.CostEstimate(
            flops=0, transcendentals=0,
            bytes_accessed=2 * tiles * share * ff_tile * source.dtype.itemsize,
        ),
        name="pack",
    )(which.reshape(1).astype(jnp.int32), rows.astype(jnp.int32), cols.astype(jnp.int32), source)


def pack_scaled(first, second, picked, core, factor, shape):
    tiles, cap, height, side, share, ff_tile = shape
    across = ff_tile // side
    half = tiles // 2

    def kernel(core_ref, row_ref, col_ref, first_ref, second_ref, out_ref):
        tile = pl.program_id(0)
        base = tile * cap
        swapped = (tile >= half).astype(jnp.int32) != core_ref[0]

        def run(in_ref):
            def block(s):
                row = pl.multiple_of(row_ref[base + s], height)
                col = pl.multiple_of(col_ref[base + s], side)
                return in_ref[pl.ds(row, height), pl.ds(col, side)]

            top = lax.fori_loop(
                0, cap, lambda s, top: jnp.maximum(top, jnp.abs(block(s))),
                jnp.zeros((height, side), F32),
            )
            top = jnp.full((16, side), jnp.max(top) * factor, F32)
            power = jnp.ceil(jnp.log2(jnp.where(top > 0, top, 1.0)))
            power = jnp.clip(power, -110.0, 110.0) - 12.0
            scale = jnp.exp2(-power)[:1] * factor

            @pl.loop(0, cap)
            def _(s):
                out_ref[0, pl.ds(pl.multiple_of(s * height, height), height)] = block(s) * scale

            out_ref[0, cap * height:] = power

        pl.when(jnp.logical_not(swapped))(lambda: run(first_ref))
        pl.when(swapped)(lambda: run(second_ref))

    def spot_of(second_half):
        def index(t, w, r, c):
            spot = (t + w[0] * half) % tiles
            return (jnp.clip(spot - half, 0, half - 1) if second_half else jnp.minimum(spot, half - 1), 0)

        return pl.BlockSpec((share, ff_tile), index)

    picked = picked.reshape(-1)
    rows, cols = (picked // across) * height, (picked % across) * side
    return pl.pallas_call(
        kernel,
        out_shape=jax.ShapeDtypeStruct((tiles, cap * height + 16, side), F32),
        grid_spec=pltpu.PrefetchScalarGridSpec(
            num_scalar_prefetch=3,
            grid=(tiles,),
            in_specs=[spot_of(False), spot_of(True)],
            out_specs=pl.BlockSpec((1, cap * height + 16, side), lambda t, w, r, c: (t, 0, 0)),
        ),
        cost_estimate=pl.CostEstimate(
            flops=0, transcendentals=0, bytes_accessed=8 * tiles * share * ff_tile,
        ),
        name="pack_scaled",
    )(core.reshape(1).astype(jnp.int32), rows.astype(jnp.int32), cols.astype(jnp.int32), first, second)


def unpack(blocks, table, share, ff_tile):
    tiles, cap, height, side = blocks.shape
    across = ff_tile // side
    n = table.shape[1]

    def kernel(table_ref, in_ref, out_ref):
        base = pl.program_id(0) * n

        @pl.loop(0, n)
        def _(p):
            slot = table_ref[base + p]
            value = in_ref[0, jnp.maximum(slot, 0)]
            out_ref[place(p, across, height, side)] = jnp.where(slot >= 0, value, jnp.zeros_like(value))

    return pl.pallas_call(
        kernel,
        out_shape=jax.ShapeDtypeStruct((share, tiles * ff_tile), blocks.dtype),
        grid_spec=pltpu.PrefetchScalarGridSpec(
            num_scalar_prefetch=1,
            grid=(tiles,),
            in_specs=[pl.BlockSpec((1, cap, height, side), lambda t, s: (t, 0, 0, 0))],
            out_specs=pl.BlockSpec((share, ff_tile), lambda t, s: (0, t)),
        ),
        cost_estimate=pl.CostEstimate(
            flops=0, transcendentals=0, bytes_accessed=8 * tiles * share * ff_tile,
        ),
        name="unpack",
    )(table.reshape(-1).astype(jnp.int32), blocks)


def accumulate(total, features, items, share, ff_tile, out_type):
    tokens = features.shape[1]
    cut, n = items[0][2].shape
    parts = [part.shape[1] for part in items[0][3]]
    height, side = items[0][3][0].shape[2:]
    across = ff_tile // side
    direct = share % 128 == 0
    together = min(cut, max(1, 256 // share))
    depth = together * share
    step = min(tokens, 256)
    steps = cut // together
    many = len(items)

    def kernel(index_ref, table_ref, *refs):
        lefts, (total_ref, out_ref, strip, sums) = refs[:many], refs[-4:]
        blocks = refs[many:-4]

        @pl.when(pl.program_id(0) == 0)
        def _():
            sums[...] = total_ref[...]

        def kept(stream, t, slot):
            own = blocks[stream * len(parts):(stream + 1) * len(parts)]
            value = own[0][t, jnp.clip(slot, 0, parts[0] - 1)]
            before = parts[0]
            for size, ref in zip(parts[1:], own[1:]):
                later = ref[t, jnp.clip(slot - before, 0, size - 1)]
                value = jnp.where(slot >= before, later, value)
                before += size
            return jnp.where(slot >= 0, value, jnp.zeros_like(value))

        for stream in range(many):
            for t in range(together):
                base = (stream * cut + pl.program_id(0) * together + t) * n

                @pl.loop(0, n)
                def _(p):
                    rows, cols = place(p, across, height, side)
                    rows = pl.ds(pl.multiple_of(t * share + rows.start, height), height)
                    strip[stream, rows, cols] = kept(stream, t, table_ref[base + p])

        @pl.loop(0, tokens // step)
        def _(m):
            at = pl.ds(pl.multiple_of(m * step, step), step)
            value = sums[at]
            for stream in range(many):
                for t in range(together if direct else 1):
                    size = share if direct else depth
                    value += jnp.dot(
                        lefts[stream][t, at], strip[stream, t * size:(t + 1) * size],
                        preferred_element_type=F32,
                    )
            sums[at] = value

        @pl.when(pl.program_id(0) == steps - 1)
        def _():
            out_ref[...] = sums[...].astype(out_type)

    def left(stream):
        first = items[stream][1] * steps
        if direct:
            return pl.BlockSpec((together, tokens, share), lambda i, e, s: (first + i, 0, e[stream]))
        return pl.BlockSpec((1, tokens, depth), lambda i, e, s: (e[stream], 0, first + i))

    def block(size, first):
        return pl.BlockSpec(
            (together, size, height, side), lambda i, e, s: (first // together + i, 0, 0, 0)
        )

    whole = pl.BlockSpec((tokens, ff_tile), lambda i, e, s: (0, 0), pipeline_mode=pl.Buffered(1))
    return pl.pallas_call(
        kernel,
        out_shape=jax.ShapeDtypeStruct((tokens, ff_tile), out_type),
        grid_spec=pltpu.PrefetchScalarGridSpec(
            num_scalar_prefetch=2,
            grid=(steps,),
            in_specs=[left(i) for i in range(many)]
            + [block(size, item[4]) for item in items for size in parts] + [whole],
            out_specs=pl.BlockSpec((tokens, ff_tile), lambda i, e, s: (0, 0)),
            scratch_shapes=[
                pltpu.VMEM((many, depth, ff_tile), BF16), pltpu.VMEM((tokens, ff_tile), F32)
            ],
        ),
        cost_estimate=pl.CostEstimate(
            flops=2 * tokens * many * cut * share * ff_tile, transcendentals=0,
            bytes_accessed=2 * tokens * many * cut * share + 8 * tokens * ff_tile,
        ),
        name="accumulate",
    )(
        jnp.stack([item[0] for item in items]).astype(jnp.int32),
        jnp.concatenate([item[2].reshape(-1) for item in items]).astype(jnp.int32),
        *[features] * many, *[part for item in items for part in item[3]], total,
    )


def pairs(count, flip):
    return [(i, i ^ flip) for i in range(count)]


def body(grad_out, acts, weight, block_mask):
    groups = lax.axis_size("dp")
    tiles = lax.axis_size("tensor")
    group = lax.axis_index("dp")
    position = lax.axis_index("tensor")
    tokens, d_tile = grad_out.shape
    ff_tile = acts.shape[1]
    side = weight.shape[1] // block_mask.shape[1]
    share = d_tile // groups
    per = tiles // groups
    rows = per * d_tile
    height = min(side, share)
    down, across = share // height, ff_tile // side
    n = down * across
    cap = -(-3 * n // 4)
    parts = [cap // 2, cap - cap // 2] if cap > 1 else [cap]
    shape = (tiles, cap, height, side, share, ff_tile)

    units = jnp.repeat(block_mask, side // height, axis=0)
    by_weight = units.reshape(tiles, groups, down, tiles, across)
    by_output = units.reshape(groups, tiles, down, tiles, across)
    turns = -(-jnp.maximum(jnp.max(jnp.sum(by_weight, (2, 4))), jnp.max(jnp.sum(by_output, (2, 4)))) // cap)

    def at(array, *where):
        for axis, index in where:
            array = lax.dynamic_index_in_dim(array, index, axis, keepdims=True)
        return array

    weight_out = at(by_weight, (0, position), (1, group))[0, 0].transpose(1, 0, 2).reshape(tiles, n)
    weight_in = at(by_weight, (3, position))[:, :, :, 0].transpose(1, 0, 2, 3).reshape(groups, tiles, n)
    result_out = at(by_output, (0, group), (3, position))[0, :, :, 0].reshape(tiles, n)
    result_in = at(by_output, (0, group), (1, position))[0, 0].transpose(1, 0, 2).reshape(tiles, n)

    def hops(array, flips, axis="dp", count=groups):
        return [lax.ppermute(array(f), axis, pairs(count, f)) for f in flips]

    acts_x, acts_y = hops(lambda f: acts, (1, 2))
    acts_low = lax.ppermute(acts_x[:tokens // 2], "dp", pairs(groups, 2))
    acts_high = lax.ppermute(acts_y[tokens // 2:], "dp", pairs(groups, 1))
    features = lax.all_gather(grad_out, "tensor", axis=0, tiled=False)

    def packed_weight(turn):
        made, first = [], turn * cap
        for size in parts:
            picked = slots_to_send(weight_out, size, first)
            made.append(pack(weight, picked, group, (tiles, size) + shape[2:]))
            first = first + size
        return made

    def exchange(array):
        return lax.all_to_all(array, "tensor", split_axis=0, concat_axis=0, tiled=True)

    own = packed_weight(0)
    own, features = lax.optimization_barrier((own, features))
    for i, part in enumerate(own):
        own[i] = exchange(part)

    core = position % 2
    half = per // 2

    def chosen(flip, which=core):
        start = (group ^ flip) * per + which * half
        return lax.dynamic_slice_in_dim(features, start, half, 0)

    got, other = [], []
    for flip in (1, 2, 3):
        got += hops(chosen, (flip,))
        other.append(lax.ppermute(got[-1], "tensor", pairs(tiles, 1)))

    def contract(left, right):
        out = jnp.einsum("ptf,th->pfh", left, right, preferred_element_type=F32)
        return out.reshape(rows // 2, ff_tile)

    products = []
    for pieces in ([chosen(0)] + got, [chosen(0, 1 - core)] + other):
        product = contract(pieces[0], acts)
        product = product + contract(pieces[1], acts_x)
        product = product + contract(pieces[2], acts_y)
        product = product + contract(pieces[3], jnp.concatenate([acts_low, acts_high], 0))
        products.append(product)
    scale_factor = 1.0 / (tokens * groups) ** 0.5

    def moved_product(turn):
        picked = slots_to_send(result_out, cap, turn * cap)
        sent = pack_scaled(*products, picked, core, scale_factor, shape).astype(jnp.float16)
        got = exchange(sent)
        power = got[:, cap * height, 0].astype(F32)
        blocks = got[:, :cap * height].astype(F32) * jnp.exp2(power)[:, None, None]
        blocks = blocks.reshape(tiles, cap, height, side)
        return unpack(blocks, slots_received(result_in, cap, turn), share, ff_tile)

    grad_weight = moved_product(0)

    if share % 128 == 0:
        lefts = features
    else:
        lefts = features.reshape(tiles, tokens, groups, share).transpose(2, 1, 0, 3)
        lefts = lefts.reshape(groups, tokens, tiles * share)
    cut = tiles // 2

    def halves(index, sources, turn):
        table = slots_received(lax.dynamic_index_in_dim(weight_in, index, 0, keepdims=False), cap, turn)
        return [(index, i, table[i * cut:(i + 1) * cut], *source) for i, source in enumerate(sources)]

    def add(total, items, out_type=F32):
        return accumulate(total, lefts, items, share, ff_tile, out_type)

    def more_acts(carry):
        turn, total = carry
        pieces = [lax.all_gather(exchange(p), "dp", axis=0, tiled=False) for p in packed_weight(turn)]

        def one(e, total):
            piece = [lax.dynamic_index_in_dim(p, e, 0, keepdims=False) for p in pieces]
            return add(total, halves(e, ((piece, 0), (piece, cut)), turn))

        return turn + 1, lax.fori_loop(0, groups, one, total)

    def more_weight(carry):
        turn, total = carry
        return turn + 1, total + moved_product(turn)

    def unfinished(carry):
        return carry[0] < turns

    total = jnp.zeros((tokens, ff_tile), F32)
    _, total = lax.while_loop(unfinished, more_acts, (jnp.int32(1), total))
    _, grad_weight = lax.while_loop(unfinished, more_weight, (jnp.int32(1), grad_weight))

    near_x, near_y, far_low, far_high = [], [], [], []
    for part in own:
        x, y = hops(lambda f: part, (1, 2))
        far_low.append(lax.ppermute(x[:cut], "dp", pairs(groups, 2)))
        far_high.append(lax.ppermute(y[cut:], "dp", pairs(groups, 1)))
        near_x.append(x)
        near_y.append(y)
    total = add(total, halves(group, ((own, 0), (own, cut)), 0))
    near = halves(group ^ 1, ((near_x, 0), (near_x, cut)), 0)
    near += halves(group ^ 2, ((near_y, 0), (near_y, cut)), 0)
    total = add(total, near)
    total = add(total, halves(group ^ 3, ((far_low, 0), (far_high, 0)), 0), BF16)
    return total, grad_weight


def solution(mesh):
    in_specs = (P("dp", "tensor"), P("dp", "tensor"), P("tensor", None), P())
    out_specs = (P("dp", "tensor"), P(("dp", "tensor"), None))
    return jax.shard_map(body, mesh=mesh, in_specs=in_specs, out_specs=out_specs, check_vma=False)
```
